32 devices in a mesh: groups: 2 (over x), mem: 16 (over z, y, core).
Axes of the slice: x: 2, y: 2, z: 4, core: 2. Of those that a mesh axis runs over, the one named last changes fastest.
Arguments:
- mem_key: bfloat16 [128, 128, 128], P(('groups', 'mem')), parts along dimension 0, may hold values from -6 to 6
- value_base: bfloat16 [128, 128, 512], P(('groups', 'mem')), parts along dimension 0, may hold values from -6 to 6
- memory_labels: int32 [128, 128], P(('groups', 'mem')), parts along dimension 0, may hold values from 0 to 7
- valid_counts: int32 [32], P(('groups', 'mem')), parts along dimension 0, may hold values from 128 to 512, as said below
- query_key: bfloat16 [32, 64, 128], P(('groups', 'mem')), parts along dimension 0, may hold values from -96 to 96
- query_value: bfloat16 [32, 64, 512], P(('groups', 'mem')), parts along dimension 0, may hold values from -6 to 6
- object_embed: bfloat16 [8, 512], replicated, may hold values from -6 to 6
- decode_weight: bfloat16 [3, 3, 1024, 256], replicated, may hold values from -0.0625 to 0.0625
- mask_weight: bfloat16 [256, 8], replicated, may hold values from -0.375 to 0.375
Outputs:
- mask_logits: float32 [32, 64, 8], P(('groups', 'mem')), parts along dimension 0
The draws below stay inside these ranges and needn't reach their ends.
There are 2 independent parts, one for each index of `groups`. The reference program is written for one: setup_inputs(seed, part) draws one part's arguments, and reference() takes and returns one part's arrays. A program takes and returns all parts, laid end to end along the dimension named above; an argument that names none is the same for every part. Nothing has to cross between parts.
Inputs may be any that keep to these rules, and one draw needn't show every extreme that they name: `valid_counts`: live positions of each memory block; some block is full and some holds a quarter.
All inputs are finite; a program needn't handle non-finite values.
Results may differ from the reference program's by a relative error of at most 0.0048.
Values may be sent and summed in bfloat16 or wider, within the bound.
No kernel may reach another device: no remote copies, remote signals or barrier semaphores. Data moves between devices by JAX's collectives and lax.ppermute only.
A program may use at most 320 MiB of HBM per device.

```python
import math
import jax
import jax.numpy as jnp
from jax import lax

KEY = 128
VAL = 512
DEC = 256
OBJ = 8
MCOLS = 128
QW = 64
MROWS = 4
MEM_ROWS = 64
QH = 16
N_MEM = 16


def draw_valid_counts(key, part):
    base_key = jax.random.fold_in(key, 11)
    first_key, second_key = jax.random.split(base_key)
    block_size = MROWS * MCOLS
    counts = jax.random.randint(first_key, (N_MEM,), block_size // 4, block_size + 1)
    order = jax.random.permutation(second_key, N_MEM)
    counts = counts.at[order[0]].set(block_size)
    counts = counts.at[order[1]].set(block_size // 4)
    return counts.astype(jnp.int32)


def draw_query_key(key, part):
    base_key = jax.random.fold_in(key, 23)
    first_key = jax.random.fold_in(base_key, 0)
    shape = (QH, QW, KEY)
    codes = jnp.clip(3.0 * jax.random.normal(first_key, shape, jnp.float32), -12.0, 12.0)
    return codes.astype(jnp.bfloat16)


def touch_ends(array, rng, low, top_value):
    shape = array.shape
    spot = [jax.random.randint(jax.random.fold_in(rng, axis), (), 0, shape[axis]) for axis in range(len(shape))]
    array = array.at[tuple(spot)].set(low)
    longest = shape.index(max(shape))
    spot[longest] = (spot[longest] + 1) % shape[longest]
    return array.at[tuple(spot)].set(top_value)


def shard_levels(stream_key, shape, pieces, least, high):
    loudness = 1.0
    for axis_at, blocks in pieces:
        heights = jax.random.uniform(jax.random.fold_in(jax.random.fold_in(stream_key, 6), axis_at), (blocks,), jnp.float32, least / len(pieces), high / len(pieces))
        loudness = loudness * jnp.repeat(jnp.exp(heights), shape[axis_at] // blocks).reshape((-1,) + (1,) * (len(shape) - 1 - axis_at))
    return loudness


def centred(key, shape, scale, bound, cuts=(), held_as=jnp.bfloat16):
    result = jax.random.normal(key, shape, jnp.float32) * scale
    if len(cuts) > 0:
        result = shard_levels(key, shape, cuts, -0.22, 0.18) * result
    return jnp.clip(result, min=-bound, max=bound).astype(held_as)


def setup_inputs(seed: int = 0, part: int = 0) -> dict:
    keys = jax.random.split(jax.random.key(seed), 10)
    part_keys = jax.random.split(jax.random.fold_in(keys[9], part), 10)
    return {
        "mem_key": centred(part_keys[0], (MEM_ROWS, MCOLS, KEY), 1.0, 6.0, ((0, 16),)),
        "value_base": centred(part_keys[1], (MEM_ROWS, MCOLS, VAL), 1.0, 6.0, ((0, 16),)),
        "memory_labels": touch_ends(jax.random.randint(part_keys[2], (MEM_ROWS, MCOLS), 0, OBJ), jax.random.fold_in(part_keys[2], 1), 0, OBJ - 1).astype(jnp.int32),
        "valid_counts": draw_valid_counts(jax.random.fold_in(jax.random.fold_in(keys[9], part), 71), part),
        "query_key": draw_query_key(jax.random.fold_in(jax.random.fold_in(keys[9], part), 71), part),
        "query_value": centred(part_keys[5], (QH, QW, VAL), 1.0, 6.0, ((0, 16),)),
        "object_embed": centred(keys[6], (OBJ, VAL), 1.0, 6.0),
        "decode_weight": centred(keys[7], (3, 3, 2 * VAL, DEC), (18 * VAL) ** -0.5, 0.0625),
        "mask_weight": centred(keys[8], (DEC, OBJ), DEC ** -0.5, 0.375),
    }


def conv_taps(padded, weight, height, width):
    summed = jnp.zeros((height * width, weight.shape[3]), jnp.float32)
    for row_step in range(3):
        for col_step in range(3):
            window = padded[row_step:row_step + height, col_step:col_step + width].reshape(height * width, -1)
            summed = summed + jnp.dot(window, weight[row_step, col_step], preferred_element_type=jnp.float32)
    return summed

def reference(mem_key, value_base, memory_labels, valid_counts, query_key, query_value, object_embed, decode_weight, mask_weight):
    block_size = MROWS * MCOLS
    onehot = (memory_labels.reshape(-1)[:, None] == jnp.arange(OBJ, dtype=jnp.int32)[None, :]).astype(jnp.bfloat16)
    embedded = jnp.dot(onehot, object_embed, preferred_element_type=jnp.float32)
    mem_value = (value_base.reshape(-1, VAL).astype(jnp.float32) + embedded).astype(jnp.bfloat16)
    keys_all = mem_key.reshape(N_MEM, block_size, KEY)
    mem_value = mem_value.reshape(N_MEM, block_size, VAL)
    queries = query_key.reshape(-1, KEY)
    score_scale = 1.0 / math.sqrt(KEY)

    def block(inputs):
        block_keys, block_vals, live_count = inputs
        scores = jnp.dot(queries, block_keys.T, preferred_element_type=jnp.float32) * score_scale
        is_live = (jnp.arange(block_size, dtype=jnp.int32) < live_count)[None, :]
        scores = jnp.where(is_live, scores, -jnp.inf)
        block_peak = lax.optimization_barrier(jnp.max(scores, axis=1))
        weights = jnp.where(is_live, jnp.exp(scores - block_peak[:, None]), 0.0).astype(jnp.bfloat16)
        block_mass = lax.optimization_barrier(jnp.sum(weights.astype(jnp.float32), axis=1))
        block_values = jnp.dot(weights, block_vals, preferred_element_type=jnp.float32)
        return (block_peak, block_mass, block_values)
    block_peak, block_mass, block_values = lax.map(block, (keys_all, mem_value, valid_counts))
    largest = lax.optimization_barrier(jnp.max(block_peak, axis=0))
    rescale = jnp.exp(block_peak - largest[None, :])
    weight_sum = lax.optimization_barrier(jnp.sum(rescale * block_mass, axis=0))
    value_sums = lax.optimization_barrier(jnp.sum(rescale[:, :, None] * block_values, axis=0))
    readout = (value_sums / weight_sum[:, None]).astype(jnp.bfloat16).reshape(QH, QW, VAL)
    joined = jnp.concatenate([readout, query_value], axis=-1)
    padded = jnp.pad(joined, ((1, 1), (1, 1), (0, 0)))
    hidden = jax.nn.relu(conv_taps(padded, decode_weight, QH, QW)).astype(jnp.bfloat16)
    logits = jnp.dot(hidden, mask_weight, preferred_element_type=jnp.float32)
    return logits.reshape(QH, QW, OBJ)
```

```python
import functools
import math

import jax
import jax.numpy as jnp
from jax import lax
from jax.experimental import pallas as pl
from jax.experimental.pallas import tpu as pltpu
from jax.sharding import PartitionSpec as P

F32 = jnp.float32
BF16 = jnp.bfloat16
PAD = 16
VM = pl.BlockSpec(memory_space=pltpu.VMEM)
SM = pl.BlockSpec(memory_space=pltpu.SMEM)


def call(kernel, out, ins, flops=0, exps=0):
    size = lambda a: math.prod(a.shape) * jnp.dtype(a.dtype).itemsize
    outs = out if isinstance(out, (tuple, list)) else (out,)
    moved = sum(size(a) for a in ins) + sum(size(a) for a in outs)
    return pl.pallas_call(
        kernel,
        out_shape=out,
        in_specs=[SM if a.ndim == 1 and a.dtype == jnp.int32 else VM for a in ins],
        out_specs=jax.tree.map(lambda _: VM, out),
        cost_estimate=pl.CostEstimate(flops=flops, transcendentals=exps, bytes_accessed=moved),
        compiler_params=pltpu.CompilerParams(vmem_limit_bytes=24 << 20),
    )(*ins)


def prep_kernel(key_ref, val_ref, lab_ref, count_ref, emb_ref, out_ref):
    pos, width = val_ref.shape
    kwidth = key_ref.shape[1]
    count = count_ref[0]
    chunk = lab_ref.shape[1]
    objects = emb_ref.shape[0]
    out_ref[...] = jnp.zeros_like(out_ref)
    live_row = lax.broadcasted_iota(jnp.int32, (pos, kwidth), 0) < count
    keys = key_ref[...].astype(F32)
    keys = jnp.where(live_row, keys, jnp.broadcast_to(keys[0:1], keys.shape))
    out_ref[0:pos, pos : pos + kwidth] = keys.astype(BF16)
    for i in range(pos // chunk):
        ids = jnp.broadcast_to(lab_ref[i : i + 1, :], (objects, chunk))
        onehot = (ids == lax.broadcasted_iota(jnp.int32, (objects, chunk), 0)).astype(F32)
        embedded = lax.dot_general(
            emb_ref[...].astype(F32), onehot, (((0,), (0,)), ((), ())), preferred_element_type=F32
        )
        value = val_ref[i * chunk : (i + 1) * chunk, :].astype(F32).T + embedded
        lane = lax.broadcasted_iota(jnp.int32, (width, chunk), 1) + i * chunk
        value = jnp.where(lane < count, value, 0.0)
        out_ref[0:width, i * chunk : (i + 1) * chunk] = value.astype(BF16)
        tail = lax.broadcasted_iota(jnp.int32, (PAD, chunk), 0)
        lane = lax.broadcasted_iota(jnp.int32, (PAD, chunk), 1) + i * chunk
        out_ref[width : width + PAD, i * chunk : (i + 1) * chunk] = jnp.where(
            (tail == 0) & (lane < count), 1.0, 0.0
        ).astype(BF16)


def pack_tail(peak, mass):
    row = lax.broadcasted_iota(jnp.int32, (PAD, peak.shape[1]), 0)
    high = mass.astype(BF16).astype(F32)
    low = mass - high
    out = jnp.where(row == 0, peak, jnp.where(row == 1, high, jnp.where(row == 2, low, 0.0)))
    return out.astype(BF16)


def keep_tail(peak, mass):
    row = lax.broadcasted_iota(jnp.int32, (PAD, peak.shape[1]), 0)
    return jnp.where(row == 0, peak, jnp.where(row == 1, mass, 0.0))


def attend(blocks, queries, pos, kwidth, width):
    scale = 1.0 / math.sqrt(kwidth)
    parts = []
    for ref in blocks:
        keys = ref[0:pos, pos : pos + kwidth]
        scores = (
            lax.dot_general(keys, queries, (((1,), (1,)), ((), ())), preferred_element_type=F32)
            * scale
        )
        peak = jnp.max(scores, axis=0, keepdims=True)
        weights = jnp.exp(scores - peak).astype(BF16)
        values = jnp.dot(ref[0 : width + PAD, 0:pos], weights, preferred_element_type=F32)
        parts.append((peak, values))
    (peak0, values0), (peak1, values1) = parts
    peak = jnp.maximum(peak0, peak1).astype(BF16).astype(F32)
    values = values0 * jnp.exp(peak0 - peak) + values1 * jnp.exp(peak1 - peak)
    return peak, values


def attend_kernel(pos, kwidth, width, send, mine_ref, other_ref, q_ref, out_ref):
    peak, values = attend((mine_ref, other_ref), q_ref[...], pos, kwidth, width)
    mass = values[width : width + 1]
    out_ref[0:width] = values[0:width].astype(out_ref.dtype)
    out_ref[width : width + PAD] = (pack_tail if send else keep_tail)(peak, mass)


def merged(width, keep_ref, got_ref):
    got_peak = got_ref[width : width + PAD].astype(F32)
    peak, mass = keep_ref[width : width + 1], keep_ref[width + 1 : width + 2]
    got_mass = got_peak[1:2] + got_peak[2:3]
    got_peak = got_peak[0:1]
    top = jnp.maximum(peak, got_peak)
    a, b = jnp.exp(peak - top), jnp.exp(got_peak - top)
    values = keep_ref[0:width] * a + got_ref[0:width].astype(F32) * b
    return values, top, mass * a + got_mass * b


def fold_kernel(width, keep_ref, got_ref, send_out, keep_out):
    values, peak, mass = merged(width, keep_ref, got_ref)
    half = values.shape[1] // 2
    if half % 128 == 0:
        send_out[0:width] = values[:, half:].astype(BF16)
        send_out[width : width + PAD] = pack_tail(peak[:, half:], mass[:, half:])
        keep_out[0:width] = values[:, :half]
        keep_out[width : width + PAD] = keep_tail(peak[:, :half], mass[:, :half])
        return
    rows = width // 2
    low, high = values[0:rows], values[rows:]
    lane = lax.broadcasted_iota(jnp.int32, (1, 2 * half), 1) < half
    swap = lambda x: pltpu.roll(x, half, 1)
    first = lambda x: jnp.where(lane, x, swap(x))
    second = lambda x: jnp.where(lane, swap(x), x)
    peak8, mass8 = (jnp.broadcast_to(x, (8, 2 * half)) for x in (peak, mass))
    send_out[0:rows] = jnp.where(lane, swap(low), high).astype(BF16)
    send_out[rows : rows + PAD] = pack_tail(second(peak8)[0:1], second(mass8)[0:1])
    keep_out[0:rows] = jnp.where(lane, low, swap(high))
    keep_out[rows : rows + PAD] = keep_tail(first(peak8)[0:1], first(mass8)[0:1])


def readout_kernel(rows, keep_ref, got_ref, out_ref):
    values, _, mass = merged(rows, keep_ref, got_ref)
    turned = (values / mass).T
    half = turned.shape[0] // 2
    out_ref[:, 0:rows] = turned[0:half].astype(BF16)
    out_ref[:, rows : 2 * rows] = turned[half:].astype(BF16)


def slide(left, right):
    rows = left.shape[0]
    row = lax.broadcasted_iota(jnp.int32, left.shape, 0)
    left = jnp.where(row == 0, 0.0, pltpu.roll(left, 1, 0))
    right = jnp.where(row == rows - 1, 0.0, pltpu.roll(right, rows - 1, 0))
    return left + right


def taps(lines, w_ref, channel):
    total = []
    for col in range(3):
        acc = None
        for row, line in lines:
            term = jnp.dot(line, w_ref[row, col, channel], preferred_element_type=F32)
            acc = term if acc is None else acc + term
        total.append(acc)
    return slide(total[0], total[2]) + total[1]


def ends(odd_ref, near_ref, far_ref):
    odd = odd_ref[0] == 1
    near, far = near_ref[...], far_ref[...]
    return jnp.where(odd, near, far), jnp.where(odd, far, near)


def query_conv_kernel(odd_ref, near_ref, far_ref, mid_ref, w_ref, out_ref):
    up, down = ends(odd_ref, near_ref, far_ref)
    width = mid_ref.shape[1]
    channel = slice(width, 2 * width)
    out_ref[...] = taps(((0, up), (1, mid_ref[...]), (2, down)), w_ref, channel)


def mid_conv_kernel(sum_ref, mid_ref, w_ref, out_ref):
    width = mid_ref.shape[1]
    out_ref[...] = sum_ref[...] + taps(((1, mid_ref[...]),), w_ref, slice(0, width))


def last_kernel(odd_ref, sum_ref, near_ref, far_ref, w_ref, mask_ref, out_ref):
    up, down = ends(odd_ref, near_ref, far_ref)
    width = up.shape[1]
    total = sum_ref[...] + taps(((0, up), (2, down)), w_ref, slice(0, width))
    hidden = jnp.maximum(total, 0.0).astype(BF16)
    out_ref[...] = jnp.dot(hidden, mask_ref[...], preferred_element_type=F32)


def shards(
    count,
    mem_key,
    value_base,
    memory_labels,
    valid_counts,
    query_key,
    query_value,
    object_embed,
    decode_weight,
    mask_weight,
):
    S = jax.ShapeDtypeStruct
    kwidth, width = mem_key.shape[2], value_base.shape[2]
    pos = mem_key.shape[0] * mem_key.shape[1]
    tall = max(pos, width) + PAD
    owned = query_value.shape[0] * query_value.shape[1]
    out_width = decode_weight.shape[3]

    def swap(x, mask):
        return lax.ppermute(x, "mem", [(i, i ^ mask) for i in range(count)])

    near_by = lambda x: swap(x, 1)
    links = [(i, i + 1) for i in range(1, count - 1, 2)]
    links = links + [(b, a) for a, b in links]
    far_by = lambda x: lax.ppermute(x, "mem", links)

    masks = [1 << i for i in range(1, count.bit_length() - 1)]
    if len(masks) > 1:
        masks[0], masks[1] = masks[1], masks[0]

    queries = query_key.reshape(owned, kwidth)
    frame = query_value.reshape(owned, width)
    odd = lax.bitwise_and(lax.axis_index("mem"), 1).reshape(1).astype(jnp.int32)

    mine = call(
        prep_kernel,
        S((tall, pos + kwidth), BF16),
        (
            mem_key.reshape(pos, kwidth),
            value_base.reshape(pos, width),
            memory_labels,
            valid_counts,
            object_embed,
        ),
        flops=2 * pos * width * 8,
    )
    other = near_by(mine)

    for mask in masks[:0:-1]:
        queries = jnp.concatenate([queries, swap(queries, mask)], axis=0)
    theirs = swap(queries, masks[0])

    lanes = queries.shape[0]
    work = dict(flops=4 * lanes * pos * (kwidth + width), exps=2 * lanes * pos)
    attend_call = lambda q, send, dtype: call(
        functools.partial(attend_kernel, pos, kwidth, width, send),
        S((width + PAD, lanes), dtype),
        (mine, other, q),
        **work,
    )
    keep = attend_call(queries, False, F32)
    send = attend_call(theirs, True, BF16)
    rows = width
    for mask in masks[1:]:
        got = swap(send, masks[masks.index(mask) - 1])
        lanes = lanes // 2
        if lanes % 128:
            out_rows, out_lanes = rows // 2 + PAD, 2 * lanes
        else:
            out_rows, out_lanes = rows + PAD, lanes
        send, keep = call(
            functools.partial(fold_kernel, rows),
            (S((out_rows, out_lanes), BF16), S((out_rows, out_lanes), F32)),
            (keep, got),
            flops=3 * rows * lanes,
        )
        rows = out_rows - PAD
    got = swap(send, masks[-1])
    readout = call(
        functools.partial(readout_kernel, rows),
        S((owned, width), BF16),
        (keep, got),
        flops=3 * rows * lanes,
    )

    conv_flops = 2 * owned * width * out_width * 3
    part = call(
        query_conv_kernel,
        S((owned, out_width), F32),
        (odd, near_by(frame), far_by(frame), frame, decode_weight),
        flops=3 * conv_flops,
    )
    near, far = near_by(readout), far_by(readout)
    part = call(
        mid_conv_kernel,
        S((owned, out_width), F32),
        (part, readout, decode_weight),
        flops=conv_flops,
    )
    logits = call(
        last_kernel,
        S((owned, mask_weight.shape[1]), F32),
        (odd, part, near, far, decode_weight, mask_weight),
        flops=2 * conv_flops,
    )
    return logits.reshape(query_value.shape[0], query_value.shape[1], mask_weight.shape[1])


def solution(mesh):
    split = P(("groups", "mem"))
    return jax.shard_map(
        functools.partial(shards, mesh.shape["mem"]),
        mesh=mesh,
        in_specs=(split,) * 6 + (P(),) * 3,
        out_specs=split,
        check_vma=False,
    )
```

```python
import functools
import math

import jax
import jax.numpy as jnp
from jax import lax
from jax.experimental import pallas as pl
from jax.experimental.pallas import tpu as pltpu
from jax.sharding import PartitionSpec as P


F32 = jnp.float32
BF16 = jnp.bfloat16
PAD = 16
VM = pl.BlockSpec(memory_space=pltpu.VMEM)
SM = pl.BlockSpec(memory_space=pltpu.SMEM)
HB = pl.BlockSpec(memory_space=pl.ANY)
S = jax.ShapeDtypeStruct


def call(kernel, out, ins, far=(), scratch=(), flops=0, exps=0, grant=24):
    size = lambda a: math.prod(a.shape) * jnp.dtype(a.dtype).itemsize
    outs = out if isinstance(out, (tuple, list)) else (out,)
    moved = sum(size(a) for a in ins) + sum(size(a) for a in outs)
    small = lambda a: a.ndim == 1 and a.dtype == jnp.int32
    return pl.pallas_call(
        kernel,
        out_shape=out,
        in_specs=[HB if i in far else SM if small(a) else VM for i, a in enumerate(ins)],
        out_specs=jax.tree.map(lambda _: VM, out),
        scratch_shapes=scratch,
        cost_estimate=pl.CostEstimate(flops=flops, transcendentals=exps, bytes_accessed=moved),
        compiler_params=pltpu.CompilerParams(vmem_limit_bytes=int(grant * 2**20)),
    )(*ins)


def prep_kernel(
    count_ref, key_hbm, val_hbm, lab_hbm, emb_hbm, out_ref,
    key_ref, val_ref, lab_ref, emb_ref, sems,
):
    copies = [
        pltpu.make_async_copy(src, dst, sems.at[i])
        for i, (src, dst) in enumerate(
            (
                (val_hbm, val_ref),
                (key_hbm, key_ref),
                (lab_hbm, lab_ref),
                (emb_hbm, emb_ref),
            )
        )
    ]
    for copy in copies:
        copy.start()
    pos, width = val_ref.shape
    kwidth = key_ref.shape[1]
    count = count_ref[0]
    chunk = lab_ref.shape[1]
    objects = emb_ref.shape[0]
    out_ref[...] = jnp.zeros_like(out_ref)
    for copy in copies:
        copy.wait()
    live_row = lax.broadcasted_iota(jnp.int32, (pos, kwidth), 0) < count
    keys = key_ref[...].astype(F32)
    keys = jnp.where(live_row, keys, jnp.broadcast_to(keys[0:1], keys.shape))
    out_ref[0:pos, pos : pos + kwidth] = keys.astype(BF16)
    for i in range(pos // chunk):
        ids = jnp.broadcast_to(lab_ref[i : i + 1, :], (objects, chunk))
        onehot = (ids == lax.broadcasted_iota(jnp.int32, (objects, chunk), 0)).astype(F32)
        embedded = lax.dot_general(
            emb_ref[...].astype(F32), onehot, (((0,), (0,)), ((), ())), preferred_element_type=F32
        )
        value = val_ref[i * chunk : (i + 1) * chunk, :].astype(F32).T + embedded
        lane = lax.broadcasted_iota(jnp.int32, (width, chunk), 1) + i * chunk
        value = jnp.where(lane < count, value, 0.0)
        out_ref[0:width, i * chunk : (i + 1) * chunk] = value.astype(BF16)
        tail = lax.broadcasted_iota(jnp.int32, (PAD, chunk), 0)
        lane = lax.broadcasted_iota(jnp.int32, (PAD, chunk), 1) + i * chunk
        out_ref[width : width + PAD, i * chunk : (i + 1) * chunk] = jnp.where(
            (tail == 0) & (lane < count), 1.0, 0.0
        ).astype(BF16)


def pack_tail(peak, mass):
    row = lax.broadcasted_iota(jnp.int32, (PAD, peak.shape[1]), 0)
    high = mass.astype(BF16).astype(F32)
    low = mass - high
    out = jnp.where(row == 0, peak, jnp.where(row == 1, high, jnp.where(row == 2, low, 0.0)))
    return out.astype(BF16)


def keep_tail(peak, mass):
    row = lax.broadcasted_iota(jnp.int32, (PAD, peak.shape[1]), 0)
    return jnp.where(row == 0, peak, jnp.where(row == 1, mass, 0.0))


def attend(blocks, queries, pos, kwidth, width):
    scale = 1.0 / math.sqrt(kwidth)
    parts = []
    for ref in blocks:
        keys = ref[0:pos, pos : pos + kwidth]
        scores = (
            lax.dot_general(keys, queries, (((1,), (1,)), ((), ())), preferred_element_type=F32)
            * scale
        )
        peak = jnp.max(scores, axis=0, keepdims=True)
        weights = jnp.exp(scores - peak).astype(BF16)
        values = jnp.dot(ref[0 : width + PAD, 0:pos], weights, preferred_element_type=F32)
        parts.append((peak, values))
    (peak0, values0), (peak1, values1) = parts
    peak = jnp.maximum(peak0, peak1).astype(BF16).astype(F32)
    values = values0 * jnp.exp(peak0 - peak) + values1 * jnp.exp(peak1 - peak)
    return peak, values


def attend_kernel(pos, kwidth, width, send, mine_ref, other_ref, q_ref, out_ref):
    peak, values = attend((mine_ref, other_ref), q_ref[...], pos, kwidth, width)
    mass = values[width : width + 1]
    out_ref[0:width] = values[0:width].astype(out_ref.dtype)
    out_ref[width : width + PAD] = (pack_tail if send else keep_tail)(peak, mass)


def merged(width, keep_ref, got_ref):
    got_peak = got_ref[width : width + PAD].astype(F32)
    peak, mass = keep_ref[width : width + 1], keep_ref[width + 1 : width + 2]
    got_mass = got_peak[1:2] + got_peak[2:3]
    got_peak = got_peak[0:1]
    top = jnp.maximum(peak, got_peak)
    a, b = jnp.exp(peak - top), jnp.exp(got_peak - top)
    values = keep_ref[0:width] * a + got_ref[0:width].astype(F32) * b
    return values, top, mass * a + got_mass * b


def fold_kernel(width, keep_ref, got_ref, send_out, keep_out):
    values, peak, mass = merged(width, keep_ref, got_ref)
    half = values.shape[1] // 2
    if half % 128 == 0:
        send_out[0:width] = values[:, half:].astype(BF16)
        send_out[width : width + PAD] = pack_tail(peak[:, half:], mass[:, half:])
        keep_out[0:width] = values[:, :half]
        keep_out[width : width + PAD] = keep_tail(peak[:, :half], mass[:, :half])
        return
    rows = width // 2
    low, high = values[0:rows], values[rows:]
    lane = lax.broadcasted_iota(jnp.int32, (1, 2 * half), 1) < half
    swap = lambda x: pltpu.roll(x, half, 1)
    first = lambda x: jnp.where(lane, x, swap(x))
    second = lambda x: jnp.where(lane, swap(x), x)
    peak8, mass8 = (jnp.broadcast_to(x, (8, 2 * half)) for x in (peak, mass))
    send_out[0:rows] = jnp.where(lane, swap(low), high).astype(BF16)
    send_out[rows : rows + PAD] = pack_tail(second(peak8)[0:1], second(mass8)[0:1])
    keep_out[0:rows] = jnp.where(lane, low, swap(high))
    keep_out[rows : rows + PAD] = keep_tail(first(peak8)[0:1], first(mass8)[0:1])


def readout_kernel(rows, keep_ref, got_ref, frame_ref, out_ref):
    values, _, mass = merged(rows, keep_ref, got_ref)
    turned = (values / mass).T
    half = turned.shape[0] // 2
    out_ref[:, 0:rows] = turned[0:half].astype(BF16)
    out_ref[:, rows : 2 * rows] = turned[half:].astype(BF16)
    out_ref[:, 2 * rows :] = frame_ref[...]


def join_kernel(a_ref, b_ref, out_ref):
    rows = a_ref.shape[0]
    out_ref[0:rows] = a_ref[...]
    out_ref[rows:] = b_ref[...]


def slide(left, right):
    rows = left.shape[0]
    row = lax.broadcasted_iota(jnp.int32, left.shape, 0)
    left = jnp.where(row == 0, 0.0, pltpu.roll(left, 1, 0))
    right = jnp.where(row == rows - 1, 0.0, pltpu.roll(right, rows - 1, 0))
    return left + right


def taps(lines):
    total = []
    for col in range(3):
        acc = None
        for line, weight in lines:
            term = jnp.dot(line, weight(col), preferred_element_type=F32)
            acc = term if acc is None else acc + term
        total.append(acc)
    return slide(total[0], total[2]) + total[1]


def ends(odd_ref, near_ref, far_ref):
    odd = odd_ref[0] == 1
    near, far = near_ref[...], far_ref[...]
    return jnp.where(odd, near, far), jnp.where(odd, far, near)


def mid_conv_kernel(mid_ref, w_hbm, out_ref, ends_ref, w_ref, sems):
    pairs = (
        (w_hbm.at[1], w_ref),
        (w_hbm.at[0], ends_ref.at[0]),
        (w_hbm.at[2], ends_ref.at[1]),
    )
    copies = [pltpu.make_async_copy(a, b, sems.at[i]) for i, (a, b) in enumerate(pairs)]
    for copy in copies:
        copy.start()
    copies[0].wait()
    out_ref[...] = taps(((mid_ref[...], lambda col: w_ref[col]),))
    for copy in copies[1:]:
        copy.wait()


def last_kernel(odd_ref, sum_ref, near_ref, far_ref, w_ref, mask_ref, out_ref):
    up, down = ends(odd_ref, near_ref, far_ref)
    total = sum_ref[...] + taps(
        ((up, lambda col: w_ref[0, col]), (down, lambda col: w_ref[1, col]))
    )
    hidden = jnp.maximum(total, 0.0).astype(BF16)
    out_ref[...] = lax.dot_general(
        mask_ref[...], hidden, (((1,), (1,)), ((), ())), preferred_element_type=F32
    )


def shards(
    count,
    mem_key,
    value_base,
    memory_labels,
    valid_counts,
    query_key,
    query_value,
    object_embed,
    decode_weight,
    mask_weight,
):
    kwidth, width = mem_key.shape[2], value_base.shape[2]
    pos = mem_key.shape[0] * mem_key.shape[1]
    tall = max(pos, width) + PAD
    owned = query_value.shape[0] * query_value.shape[1]
    out_width = decode_weight.shape[3]

    def swap(x, mask):
        return lax.ppermute(x, "mem", [(i, i ^ mask) for i in range(count)])

    near_by = lambda x: swap(x, 1)
    links = [(i, i + 1) for i in range(1, count - 1, 2)]
    links = links + [(b, a) for a, b in links]
    far_by = lambda x: lax.ppermute(x, "mem", links)

    masks = [1 << i for i in range(1, count.bit_length() - 1)]
    if len(masks) > 1:
        masks[0], masks[1] = masks[1], masks[0]

    queries = query_key.reshape(owned, kwidth)
    frame = query_value.reshape(owned, width)
    odd = lax.bitwise_and(lax.axis_index("mem"), 1).reshape(1).astype(jnp.int32)

    dma = pltpu.SemaphoreType.DMA
    got = swap(queries, masks[-1])
    mine = call(
        prep_kernel,
        S((tall, pos + kwidth), BF16),
        (
            valid_counts,
            mem_key.reshape(pos, kwidth),
            value_base.reshape(pos, width),
            memory_labels,
            object_embed,
        ),
        far=(1, 2, 3, 4),
        scratch=(
            pltpu.VMEM((pos, kwidth), BF16),
            pltpu.VMEM((pos, width), BF16),
            pltpu.VMEM(memory_labels.shape, jnp.int32),
            pltpu.VMEM(object_embed.shape, BF16),
            dma((4,)),
        ),
        flops=2 * pos * width * 8,
        grant=58,
    )
    other = near_by(mine)

    for mask in masks[-2::-1]:
        queries = call(
            join_kernel, S((2 * queries.shape[0], kwidth), BF16), (queries, got)
        )
        got = swap(queries, mask)
    theirs = got

    lanes = queries.shape[0]
    work = dict(flops=4 * lanes * pos * (kwidth + width), exps=2 * lanes * pos)
    attend_call = lambda q, send, dtype: call(
        functools.partial(attend_kernel, pos, kwidth, width, send),
        S((width + PAD, lanes), dtype),
        (mine, other, q),
        **work,
    )
    keep = attend_call(queries, False, F32)
    send = attend_call(theirs, True, BF16)
    conv_flops = 2 * owned * width * out_width * 3
    rows = width
    for i, mask in enumerate(masks):
        got = swap(send, mask)
        if i + 1 == len(masks):
            break
        lanes = lanes // 2
        if lanes % 128:
            out_rows, out_lanes = rows // 2 + PAD, 2 * lanes
        else:
            out_rows, out_lanes = rows + PAD, lanes
        send, keep = call(
            functools.partial(fold_kernel, rows),
            (S((out_rows, out_lanes), BF16), S((out_rows, out_lanes), F32)),
            (keep, got),
            flops=3 * rows * lanes,
        )
        rows = out_rows - PAD
    joined = call(
        functools.partial(readout_kernel, rows),
        S((owned, 2 * width), BF16),
        (keep, got, frame),
        flops=3 * rows * lanes,
    )
    far = far_by(joined)
    near = near_by(joined)
    part, end_weight = call(
        mid_conv_kernel,
        (S((owned, out_width), F32), S((2, *decode_weight.shape[1:]), BF16)),
        (joined, decode_weight),
        far=(1,),
        scratch=(pltpu.VMEM(decode_weight.shape[1:], BF16), dma((3,))),
        flops=2 * conv_flops,
        grant=50,
    )
    objects = mask_weight.shape[1]
    logits = call(
        last_kernel,
        S((objects, owned), F32),
        (odd, part, near, far, end_weight, mask_weight.T),
        flops=4 * conv_flops,
    )
    return logits.T.reshape(query_value.shape[0], query_value.shape[1], objects)


def solution(mesh):
    split = P(("groups", "mem"))
    count = mesh.shape["mem"]

    def step(*args):
        return shards(count, *args)

    return jax.shard_map(
        step,
        mesh=mesh,
        in_specs=(split,) * 6 + (P(),) * 3,
        out_specs=split,
        check_vma=False,
    )
```

```python
import functools
import math

import jax
import jax.numpy as jnp
from jax import lax
from jax.experimental import pallas as pl
from jax.experimental.pallas import tpu as pltpu
from jax.sharding import PartitionSpec as P


F32 = jnp.float32
BF16 = jnp.bfloat16
PAD = 16
VM = pl.BlockSpec(memory_space=pltpu.VMEM)
SM = pl.BlockSpec(memory_space=pltpu.SMEM)
HB = pl.BlockSpec(memory_space=pl.ANY)
S = jax.ShapeDtypeStruct
hold = pltpu.with_memory_space_constraint


def call(kernel, out, ins, far=(), scratch=(), flops=0, exps=0):
    size = lambda a: math.prod(a.shape) * jnp.dtype(a.dtype).itemsize
    outs = out if isinstance(out, (tuple, list)) else (out,)
    moved = sum(size(a) for a in ins) + sum(size(a) for a in outs)
    small = lambda a: a.ndim == 1 and a.dtype == jnp.int32
    return pl.pallas_call(
        kernel,
        out_shape=out,
        in_specs=[HB if i in far else SM if small(a) else VM for i, a in enumerate(ins)],
        out_specs=jax.tree.map(lambda _: VM, out),
        scratch_shapes=scratch,
        cost_estimate=pl.CostEstimate(flops=flops, transcendentals=exps, bytes_accessed=moved),
        compiler_params=pltpu.CompilerParams(vmem_limit_bytes=24 << 20),
    )(*[hold(a, pltpu.HBM) if i in far else a for i, a in enumerate(ins)])


def prep_kernel(
    key_hbm, val_hbm, lab_hbm, emb_hbm, q_hbm, count_ref, out_ref, q_ref,
    key_ref, val_ref, lab_ref, emb_ref, sems,
):
    pairs = (
        (val_hbm, val_ref),
        (key_hbm, key_ref),
        (lab_hbm, lab_ref),
        (emb_hbm, emb_ref),
        (q_hbm, q_ref),
    )
    copies = [pltpu.make_async_copy(a, b, sems.at[i]) for i, (a, b) in enumerate(pairs)]
    for copy in copies:
        copy.start()
    pos, width = val_ref.shape
    kwidth = key_ref.shape[1]
    chunk = lab_ref.shape[1]
    objects = emb_ref.shape[0]
    out_ref[...] = jnp.zeros_like(out_ref)
    for copy in copies:
        copy.wait()
    count = count_ref[0]
    live_row = lax.broadcasted_iota(jnp.int32, (pos, kwidth), 0) < count
    keys = key_ref[...].astype(F32)
    keys = jnp.where(live_row, keys, jnp.broadcast_to(keys[0:1], keys.shape))
    out_ref[0:pos, pos : pos + kwidth] = keys.astype(BF16)
    for i in range(pos // chunk):
        ids = jnp.broadcast_to(lab_ref[i : i + 1, :], (objects, chunk))
        onehot = (ids == lax.broadcasted_iota(jnp.int32, (objects, chunk), 0)).astype(F32)
        embedded = lax.dot_general(
            emb_ref[...].astype(F32), onehot, (((0,), (0,)), ((), ())), preferred_element_type=F32
        )
        value = val_ref[i * chunk : (i + 1) * chunk, :].astype(F32).T + embedded
        lane = lax.broadcasted_iota(jnp.int32, (width, chunk), 1) + i * chunk
        value = jnp.where(lane < count, value, 0.0)
        out_ref[0:width, i * chunk : (i + 1) * chunk] = value.astype(BF16)
        tail = lax.broadcasted_iota(jnp.int32, (PAD, chunk), 0)
        lane = lax.broadcasted_iota(jnp.int32, (PAD, chunk), 1) + i * chunk
        out_ref[width : width + PAD, i * chunk : (i + 1) * chunk] = jnp.where(
            (tail == 0) & (lane < count), 1.0, 0.0
        ).astype(BF16)


def pack_tail(peak, mass):
    row = lax.broadcasted_iota(jnp.int32, (PAD, peak.shape[1]), 0)
    high = mass.astype(BF16).astype(F32)
    low = mass - high
    out = jnp.where(row == 0, peak, jnp.where(row == 1, high, jnp.where(row == 2, low, 0.0)))
    return out.astype(BF16)


def keep_tail(peak, mass):
    row = lax.broadcasted_iota(jnp.int32, (PAD, peak.shape[1]), 0)
    return jnp.where(row == 0, peak, jnp.where(row == 1, mass, 0.0))


def attend(blocks, queries, pos, kwidth, width):
    scale = 1.0 / math.sqrt(kwidth)
    parts = []
    for ref in blocks:
        keys = ref[0:pos, pos : pos + kwidth]
        scores = (
            lax.dot_general(keys, queries, (((1,), (1,)), ((), ())), preferred_element_type=F32)
            * scale
        )
        peak = jnp.max(scores, axis=0, keepdims=True)
        weights = jnp.exp(scores - peak).astype(BF16)
        values = jnp.dot(ref[0 : width + PAD, 0:pos], weights, preferred_element_type=F32)
        parts.append((peak, values))
    (peak0, values0), (peak1, values1) = parts
    peak = jnp.maximum(peak0, peak1).astype(BF16).astype(F32)
    values = values0 * jnp.exp(peak0 - peak) + values1 * jnp.exp(peak1 - peak)
    return peak, values


def attend_kernel(pos, kwidth, width, send, mine_ref, other_ref, q_ref, out_ref):
    peak, values = attend((mine_ref, other_ref), q_ref[...], pos, kwidth, width)
    mass = values[width : width + 1]
    out_ref[0:width] = values[0:width].astype(out_ref.dtype)
    out_ref[width : width + PAD] = (pack_tail if send else keep_tail)(peak, mass)


def merged(width, keep_ref, got_ref):
    got_peak = got_ref[width : width + PAD].astype(F32)
    peak, mass = keep_ref[width : width + 1], keep_ref[width + 1 : width + 2]
    got_mass = got_peak[1:2] + got_peak[2:3]
    got_peak = got_peak[0:1]
    top = jnp.maximum(peak, got_peak)
    a, b = jnp.exp(peak - top), jnp.exp(got_peak - top)
    values = keep_ref[0:width] * a + got_ref[0:width].astype(F32) * b
    return values, top, mass * a + got_mass * b


def fold_kernel(width, keep_ref, got_ref, send_out, keep_out):
    values, peak, mass = merged(width, keep_ref, got_ref)
    half = values.shape[1] // 2
    if half % 128 == 0:
        send_out[0:width] = values[:, half:].astype(BF16)
        send_out[width : width + PAD] = pack_tail(peak[:, half:], mass[:, half:])
        keep_out[0:width] = values[:, :half]
        keep_out[width : width + PAD] = keep_tail(peak[:, :half], mass[:, :half])
        return
    rows = width // 2
    low, high = values[0:rows], values[rows:]
    lane = lax.broadcasted_iota(jnp.int32, (1, 2 * half), 1) < half
    swap = lambda x: pltpu.roll(x, half, 1)
    first = lambda x: jnp.where(lane, x, swap(x))
    second = lambda x: jnp.where(lane, swap(x), x)
    peak8, mass8 = (jnp.broadcast_to(x, (8, 2 * half)) for x in (peak, mass))
    send_out[0:rows] = jnp.where(lane, swap(low), high).astype(BF16)
    send_out[rows : rows + PAD] = pack_tail(second(peak8)[0:1], second(mass8)[0:1])
    keep_out[0:rows] = jnp.where(lane, low, swap(high))
    keep_out[rows : rows + PAD] = keep_tail(first(peak8)[0:1], first(mass8)[0:1])


def readout_kernel(rows, keep_ref, got_ref, frame_ref, out_ref):
    values, _, mass = merged(rows, keep_ref, got_ref)
    turned = (values / mass).T
    half = turned.shape[0] // 2
    out_ref[:, 0:rows] = turned[0:half].astype(BF16)
    out_ref[:, rows : 2 * rows] = turned[half:].astype(BF16)
    out_ref[:, 2 * rows :] = frame_ref[...]


def join_kernel(a_ref, b_ref, out_ref):
    rows = a_ref.shape[0]
    out_ref[0:rows] = a_ref[...]
    out_ref[rows:] = b_ref[...]


def slide(left, right):
    rows = left.shape[0]
    row = lax.broadcasted_iota(jnp.int32, left.shape, 0)
    left = jnp.where(row == 0, 0.0, pltpu.roll(left, 1, 0))
    right = jnp.where(row == rows - 1, 0.0, pltpu.roll(right, rows - 1, 0))
    return left + right


def taps(lines):
    total = []
    for col in range(3):
        acc = None
        for line, weight in lines:
            term = jnp.dot(line, weight(col), preferred_element_type=F32)
            acc = term if acc is None else acc + term
        total.append(acc)
    return slide(total[0], total[2]) + total[1]


def ends(count, near_ref, far_ref):
    place = lax.axis_index("mem")
    odd = lax.rem(place, 2) == 1
    near, far = near_ref[...], far_ref[...]
    far = jnp.where((place == 0) | (place == count - 1), jnp.zeros_like(far), far)
    return jnp.where(odd, near, far), jnp.where(odd, far, near)


def copy_all(pairs, sems):
    copies = [pltpu.make_async_copy(a, b, sems.at[i]) for i, (a, b) in enumerate(pairs)]
    for copy in copies:
        copy.start()
    return copies


def stage_kernel(w_hbm, frame_hbm, ends_ref, frame_ref, sems):
    pairs = (
        (frame_hbm, frame_ref),
        (w_hbm.at[0], ends_ref.at[0]),
        (w_hbm.at[2], ends_ref.at[1]),
    )
    for copy in copy_all(pairs, sems):
        copy.wait()


def mid_conv_kernel(mid_ref, w_hbm, out_ref, w_ref, sems):
    for copy in copy_all(((w_hbm.at[1], w_ref),), sems):
        copy.wait()
    out_ref[...] = taps(((mid_ref[...], lambda col: w_ref[col]),))


def last_kernel(count, sum_ref, near_ref, far_ref, w_ref, mask_ref, out_ref):
    up, down = ends(count, near_ref, far_ref)
    total = sum_ref[...] + taps(
        ((up, lambda col: w_ref[0, col]), (down, lambda col: w_ref[1, col]))
    )
    hidden = jnp.maximum(total, 0.0).astype(BF16)
    out_ref[...] = lax.dot_general(
        mask_ref[...], hidden, (((1,), (1,)), ((), ())), preferred_element_type=F32
    )


def shards(
    groups,
    count,
    mem_key,
    value_base,
    memory_labels,
    valid_counts,
    query_key,
    query_value,
    object_embed,
    decode_weight,
    mask_weight,
):
    kwidth, width = mem_key.shape[2], value_base.shape[2]
    pos = mem_key.shape[0] * mem_key.shape[1]
    tall = max(pos, width) + PAD
    owned = query_value.shape[0] * query_value.shape[1]
    out_width = decode_weight.shape[3]

    steps = count.bit_length() - 2
    order = [[1 << i for i in range(1, steps + 1)] for _ in range(2)]
    order[1][0:2] = order[1][1::-1]

    def swap(x, step):
        return lax.ppermute(x, "mem", [(i, i ^ order[i & 1][step]) for i in range(count)])

    def near_by(x):
        return lax.ppermute(x, "mem", [(i, i ^ 1) for i in range(count)])

    def far_by(x):
        links = []
        for group in range(groups):
            base = group * count
            links += [(base + i, base + i + 1) for i in range(1, count - 1, 2)]
            if groups % 2 == 0 and group % 2 == 0:
                links += [(base + i, base + count + i) for i in (0, count - 1)]
        links += [(b, a) for a, b in links]
        return lax.ppermute(x, ("groups", "mem"), links)

    queries = query_key.reshape(owned, kwidth)
    frame = query_value.reshape(owned, width)
    dma = pltpu.SemaphoreType.DMA
    got = swap(queries, steps - 1)
    mine, queries = call(
        prep_kernel,
        (S((tall, pos + kwidth), BF16), S(queries.shape, BF16)),
        (
            mem_key.reshape(pos, kwidth),
            value_base.reshape(pos, width),
            memory_labels,
            object_embed,
            queries,
            valid_counts,
        ),
        far=range(5),
        scratch=(
            pltpu.VMEM((pos, kwidth), BF16),
            pltpu.VMEM((pos, width), BF16),
            pltpu.VMEM(memory_labels.shape, jnp.int32),
            pltpu.VMEM(object_embed.shape, BF16),
            dma((5,)),
        ),
        flops=2 * pos * width * 8,
    )
    other = near_by(mine)

    for i in range(steps - 1):
        queries = call(
            join_kernel, S((2 * queries.shape[0], kwidth), BF16), (queries, got)
        )
        got = swap(queries, steps - 2 - i)
    theirs = got

    lanes = queries.shape[0]
    work = dict(flops=4 * lanes * pos * (kwidth + width), exps=2 * lanes * pos)
    attend_call = lambda q, send, dtype: call(
        functools.partial(attend_kernel, pos, kwidth, width, send),
        S((width + PAD, lanes), dtype),
        (mine, other, q),
        **work,
    )
    keep = attend_call(queries, False, F32)
    send = attend_call(theirs, True, BF16)
    conv_flops = 2 * owned * width * out_width * 3
    taps_shape = decode_weight.shape[1:]
    end_weight, held = call(
        stage_kernel,
        (S((2, *taps_shape), BF16), S(frame.shape, BF16)),
        (decode_weight, frame),
        far=(0, 1),
        scratch=(dma((3,)),),
    )
    rows = width
    for i in range(steps):
        got = swap(send, i)
        if i + 1 == steps:
            break
        lanes = lanes // 2
        if lanes % 128:
            out_rows, out_lanes = rows // 2 + PAD, 2 * lanes
        else:
            out_rows, out_lanes = rows + PAD, lanes
        send, keep = call(
            functools.partial(fold_kernel, rows),
            (S((out_rows, out_lanes), BF16), S((out_rows, out_lanes), F32)),
            (keep, got),
            flops=3 * rows * lanes,
        )
        rows = out_rows - PAD
    joined = call(
        functools.partial(readout_kernel, rows),
        S((owned, 2 * width), BF16),
        (keep, got, held),
        flops=3 * rows * lanes,
    )
    far = far_by(joined)
    near = near_by(joined)
    part = call(
        mid_conv_kernel,
        S((owned, out_width), F32),
        (joined, decode_weight),
        far=(1,),
        scratch=(pltpu.VMEM(taps_shape, BF16), dma((1,))),
        flops=2 * conv_flops,
    )
    objects = mask_weight.shape[1]
    logits = call(
        functools.partial(last_kernel, count),
        S((objects, owned), F32),
        (part, near, far, end_weight, mask_weight.T),
        flops=4 * conv_flops,
    )
    return logits.T.reshape(query_value.shape[0], query_value.shape[1], objects)


def solution(mesh):
    split = P(("groups", "mem"))
    count = mesh.shape["mem"]

    def step(*args):
        return shards(mesh.shape["groups"], count, *args)

    return jax.shard_map(
        step,
        mesh=mesh,
        in_specs=(split,) * 6 + (P(),) * 3,
        out_specs=split,
        check_vma=False,
    )
```

```python
import functools
import math

import jax
import jax.numpy as jnp
from jax import lax
from jax.experimental import pallas as pl
from jax.experimental.pallas import tpu as pltpu
from jax.sharding import PartitionSpec as P


F32 = jnp.float32
BF16 = jnp.bfloat16
PAD = 16
VM = pl.BlockSpec(memory_space=pltpu.VMEM)
SM = pl.BlockSpec(memory_space=pltpu.SMEM)
HB = pl.BlockSpec(memory_space=pl.ANY)
S = jax.ShapeDtypeStruct
hold = pltpu.with_memory_space_constraint


def call(kernel, out, ins, far=(), scratch=(), flops=0, exps=0):
    size = lambda a: math.prod(a.shape) * jnp.dtype(a.dtype).itemsize
    outs = out if isinstance(out, (tuple, list)) else (out,)
    moved = sum(size(a) for a in ins) + sum(size(a) for a in outs)
    small = lambda a: a.ndim == 1 and a.dtype == jnp.int32
    return pl.pallas_call(
        kernel,
        out_shape=out,
        in_specs=[HB if i in far else SM if small(a) else VM for i, a in enumerate(ins)],
        out_specs=jax.tree.map(lambda _: VM, out),
        scratch_shapes=scratch,
        cost_estimate=pl.CostEstimate(flops=flops, transcendentals=exps, bytes_accessed=moved),
        compiler_params=pltpu.CompilerParams(vmem_limit_bytes=24 << 20),
    )(*[hold(a, pltpu.HBM) if i in far else a for i, a in enumerate(ins)])


def prep_kernel(
    key_hbm, val_hbm, lab_hbm, emb_hbm, q_hbm, count_ref, out_ref, q_ref,
    key_ref, val_ref, lab_ref, emb_ref, sems,
):
    pairs = (
        (val_hbm, val_ref),
        (key_hbm, key_ref),
        (lab_hbm, lab_ref),
        (emb_hbm, emb_ref),
        (q_hbm, q_ref),
    )
    copies = [pltpu.make_async_copy(a, b, sems.at[i]) for i, (a, b) in enumerate(pairs)]
    for copy in copies:
        copy.start()
    pos, width = val_ref.shape
    kwidth = key_ref.shape[1]
    chunk = lab_ref.shape[1]
    objects = emb_ref.shape[0]
    out_ref[...] = jnp.zeros_like(out_ref)
    for copy in copies:
        copy.wait()
    count = count_ref[0]
    live_row = lax.broadcasted_iota(jnp.int32, (pos, kwidth), 0) < count
    keys = key_ref[...].astype(F32)
    keys = jnp.where(live_row, keys, jnp.broadcast_to(keys[0:1], keys.shape))
    out_ref[0:pos, pos : pos + kwidth] = keys.astype(BF16)
    for i in range(pos // chunk):
        ids = jnp.broadcast_to(lab_ref[i : i + 1, :], (objects, chunk))
        onehot = (ids == lax.broadcasted_iota(jnp.int32, (objects, chunk), 0)).astype(F32)
        embedded = lax.dot_general(
            emb_ref[...].astype(F32), onehot, (((0,), (0,)), ((), ())), preferred_element_type=F32
        )
        value = val_ref[i * chunk : (i + 1) * chunk, :].astype(F32).T + embedded
        lane = lax.broadcasted_iota(jnp.int32, (width, chunk), 1) + i * chunk
        value = jnp.where(lane < count, value, 0.0)
        out_ref[0:width, i * chunk : (i + 1) * chunk] = value.astype(BF16)
        tail = lax.broadcasted_iota(jnp.int32, (PAD, chunk), 0)
        lane = lax.broadcasted_iota(jnp.int32, (PAD, chunk), 1) + i * chunk
        out_ref[width : width + PAD, i * chunk : (i + 1) * chunk] = jnp.where(
            (tail == 0) & (lane < count), 1.0, 0.0
        ).astype(BF16)


def pack_tail(peak, mass):
    row = lax.broadcasted_iota(jnp.int32, (PAD, peak.shape[1]), 0)
    high = mass.astype(BF16).astype(F32)
    low = mass - high
    out = jnp.where(row == 0, peak, jnp.where(row == 1, high, jnp.where(row == 2, low, 0.0)))
    return out.astype(BF16)


def keep_tail(peak, mass):
    row = lax.broadcasted_iota(jnp.int32, (PAD, peak.shape[1]), 0)
    return jnp.where(row == 0, peak, jnp.where(row == 1, mass, 0.0))


def attend(blocks, queries, pos, kwidth, width):
    scale = 1.0 / math.sqrt(kwidth)
    parts = []
    for ref in blocks:
        keys = ref[0:pos, pos : pos + kwidth]
        scores = (
            lax.dot_general(keys, queries, (((1,), (1,)), ((), ())), preferred_element_type=F32)
            * scale
        )
        peak = jnp.max(scores, axis=0, keepdims=True)
        weights = jnp.exp(scores - peak).astype(BF16)
        values = jnp.dot(ref[0 : width + PAD, 0:pos], weights, preferred_element_type=F32)
        parts.append((peak, values))
    (peak0, values0), (peak1, values1) = parts
    peak = jnp.maximum(peak0, peak1).astype(BF16).astype(F32)
    values = values0 * jnp.exp(peak0 - peak) + values1 * jnp.exp(peak1 - peak)
    return peak, values


def attend_kernel(pos, kwidth, width, send, mine_ref, other_ref, q_ref, out_ref):
    peak, values = attend((mine_ref, other_ref), q_ref[...], pos, kwidth, width)
    mass = values[width : width + 1]
    out_ref[0:width] = values[0:width].astype(out_ref.dtype)
    out_ref[width : width + PAD] = (pack_tail if send else keep_tail)(peak, mass)


def merged(width, keep_ref, got_ref):
    got_peak = got_ref[width : width + PAD].astype(F32)
    peak, mass = keep_ref[width : width + 1], keep_ref[width + 1 : width + 2]
    got_mass = got_peak[1:2] + got_peak[2:3]
    got_peak = got_peak[0:1]
    top = jnp.maximum(peak, got_peak)
    a, b = jnp.exp(peak - top), jnp.exp(got_peak - top)
    values = keep_ref[0:width] * a + got_ref[0:width].astype(F32) * b
    return values, top, mass * a + got_mass * b


def fold_kernel(width, keep_ref, got_ref, send_out, keep_out):
    values, peak, mass = merged(width, keep_ref, got_ref)
    half = values.shape[1] // 2
    if half % 128 == 0:
        send_out[0:width] = values[:, half:].astype(BF16)
        send_out[width : width + PAD] = pack_tail(peak[:, half:], mass[:, half:])
        keep_out[0:width] = values[:, :half]
        keep_out[width : width + PAD] = keep_tail(peak[:, :half], mass[:, :half])
        return
    rows = width // 2
    low, high = values[0:rows], values[rows:]
    lane = lax.broadcasted_iota(jnp.int32, (1, 2 * half), 1) < half
    swap = lambda x: pltpu.roll(x, half, 1)
    first = lambda x: jnp.where(lane, x, swap(x))
    second = lambda x: jnp.where(lane, swap(x), x)
    peak8, mass8 = (jnp.broadcast_to(x, (8, 2 * half)) for x in (peak, mass))
    send_out[0:rows] = jnp.where(lane, swap(low), high).astype(BF16)
    send_out[rows : rows + PAD] = pack_tail(second(peak8)[0:1], second(mass8)[0:1])
    keep_out[0:rows] = jnp.where(lane, low, swap(high))
    keep_out[rows : rows + PAD] = keep_tail(first(peak8)[0:1], first(mass8)[0:1])


def readout_kernel(rows, keep_ref, got_ref, out_ref):
    values, _, mass = merged(rows, keep_ref, got_ref)
    turned = (values / mass).T
    half = turned.shape[0] // 2
    out_ref[:, 0:rows] = turned[0:half].astype(BF16)
    out_ref[:, rows : 2 * rows] = turned[half:].astype(BF16)


def join_kernel(a_ref, b_ref, out_ref):
    rows = a_ref.shape[0]
    out_ref[0:rows] = a_ref[...]
    out_ref[rows:] = b_ref[...]


def slide(left, right):
    rows = left.shape[0]
    row = lax.broadcasted_iota(jnp.int32, left.shape, 0)
    left = jnp.where(row == 0, 0.0, pltpu.roll(left, 1, 0))
    right = jnp.where(row == rows - 1, 0.0, pltpu.roll(right, rows - 1, 0))
    return left + right


def taps(lines):
    total = []
    for col in range(3):
        acc = None
        for line, weight in lines:
            term = jnp.dot(line, weight(col), preferred_element_type=F32)
            acc = term if acc is None else acc + term
        total.append(acc)
    return slide(total[0], total[2]) + total[1]


def ends(count, near_ref, far_ref):
    place = lax.axis_index("mem")
    odd = lax.rem(place, 2) == 1
    near, far = near_ref[...], far_ref[...]
    far = jnp.where((place == 0) | (place == count - 1), jnp.zeros_like(far), far)
    return jnp.where(odd, near, far), jnp.where(odd, far, near)


def copy_all(pairs, sems):
    copies = [pltpu.make_async_copy(a, b, sems.at[i]) for i, (a, b) in enumerate(pairs)]
    for copy in copies:
        copy.start()
    return copies


def stage_kernel(w_hbm, ends_ref, sems):
    low = pl.ds(0, ends_ref.shape[2])
    pairs = [(w_hbm.at[2 * i, :, low], ends_ref.at[i]) for i in range(2)]
    for copy in copy_all(pairs, sems):
        copy.wait()


def frame_conv_kernel(count, near_ref, far_ref, frame_hbm, w_hbm, out_ref, frame_ref, w_ref, sems):
    width = frame_ref.shape[1]
    pairs = [(frame_hbm, frame_ref)]
    pairs += [(w_hbm.at[i, :, pl.ds(width, width)], w_ref.at[i]) for i in range(3)]
    for copy in copy_all(pairs, sems):
        copy.wait()
    up, down = ends(count, near_ref, far_ref)
    lines = (up, frame_ref[...], down)
    out_ref[...] = taps([(line, functools.partial(column, w_ref, i)) for i, line in enumerate(lines)])


def column(w_ref, row, col):
    return w_ref[row, col]


def mid_conv_kernel(mid_ref, w_hbm, out_ref, w_ref, sems):
    for copy in copy_all([(w_hbm.at[1, :, pl.ds(0, w_ref.shape[1])], w_ref)], sems):
        copy.wait()
    out_ref[...] = taps([(mid_ref[...], lambda col: w_ref[col])])


def last_kernel(count, frame_sum_ref, mid_sum_ref, near_ref, far_ref, w_ref, mask_ref, out_ref):
    lines = ends(count, near_ref, far_ref)
    total = taps([(line, functools.partial(column, w_ref, i)) for i, line in enumerate(lines)])
    total = total + mid_sum_ref[...] + frame_sum_ref[...]
    hidden = jnp.maximum(total, 0.0).astype(BF16)
    out_ref[...] = lax.dot_general(
        mask_ref[...], hidden, (((1,), (1,)), ((), ())), preferred_element_type=F32
    )


def shards(
    groups,
    count,
    mem_key,
    value_base,
    memory_labels,
    valid_counts,
    query_key,
    query_value,
    object_embed,
    decode_weight,
    mask_weight,
):
    kwidth, width = mem_key.shape[2], value_base.shape[2]
    pos = mem_key.shape[0] * mem_key.shape[1]
    tall = max(pos, width) + PAD
    owned = query_value.shape[0] * query_value.shape[1]
    out_width = decode_weight.shape[3]

    steps = count.bit_length() - 2
    order = [(1 << i) + 1 for i in range(1, steps + 1)]
    order[0:2] = order[1::-1]

    def swap(x, step):
        return lax.ppermute(x, "mem", [(i, i ^ order[step]) for i in range(count)])

    def near_by(x):
        return lax.ppermute(x, "mem", [(i, i ^ 1) for i in range(count)])

    def far_by(x):
        links = []
        for group in range(groups):
            base = group * count
            links += [(base + i, base + i + 1) for i in range(1, count - 1, 2)]
            if groups % 2 == 0 and group % 2 == 0:
                links += [(base + i, base + count + i) for i in (0, count - 1)]
        links += [(b, a) for a, b in links]
        return lax.ppermute(x, ("groups", "mem"), links)

    queries = query_key.reshape(owned, kwidth)
    frame = query_value.reshape(owned, width)
    dma = pltpu.SemaphoreType.DMA
    got = swap(queries, steps - 1)
    mine, queries = call(
        prep_kernel,
        (S((tall, pos + kwidth), BF16), S(queries.shape, BF16)),
        (
            mem_key.reshape(pos, kwidth),
            value_base.reshape(pos, width),
            memory_labels,
            object_embed,
            queries,
            valid_counts,
        ),
        far=range(5),
        scratch=(
            pltpu.VMEM((pos, kwidth), BF16),
            pltpu.VMEM((pos, width), BF16),
            pltpu.VMEM(memory_labels.shape, jnp.int32),
            pltpu.VMEM(object_embed.shape, BF16),
            dma((5,)),
        ),
        flops=2 * pos * width * 8,
    )
    other = near_by(mine)

    for i in range(steps - 1):
        queries = call(
            join_kernel, S((2 * queries.shape[0], kwidth), BF16), (queries, got)
        )
        got = swap(queries, steps - 2 - i)
    theirs = got

    lanes = queries.shape[0]
    work = dict(flops=4 * lanes * pos * (kwidth + width), exps=2 * lanes * pos)
    attend_call = lambda q, send, dtype: call(
        functools.partial(attend_kernel, pos, kwidth, width, send),
        S((width + PAD, lanes), dtype),
        (mine, other, q),
        **work,
    )
    keep = attend_call(queries, False, F32)
    send = attend_call(theirs, True, BF16)
    conv_flops = 2 * owned * width * out_width * 3
    columns = decode_weight.shape[1]
    half_taps = (columns, width, out_width)
    end_weight = call(
        stage_kernel,
        S((2, *half_taps), BF16),
        (decode_weight,),
        far=(0,),
        scratch=(dma((2,)),),
    )
    frame_far = far_by(frame)
    frame_near = near_by(frame)
    frame_part = call(
        functools.partial(frame_conv_kernel, count),
        S((owned, out_width), F32),
        (frame_near, frame_far, frame, decode_weight),
        far=(2, 3),
        scratch=(pltpu.VMEM(frame.shape, BF16), pltpu.VMEM((3, *half_taps), BF16), dma((4,))),
        flops=3 * conv_flops,
    )
    rows = width
    for i in range(steps):
        got = swap(send, i)
        if i + 1 == steps:
            break
        lanes = lanes // 2
        if lanes % 128:
            out_rows, out_lanes = rows // 2 + PAD, 2 * lanes
        else:
            out_rows, out_lanes = rows + PAD, lanes
        send, keep = call(
            functools.partial(fold_kernel, rows),
            (S((out_rows, out_lanes), BF16), S((out_rows, out_lanes), F32)),
            (keep, got),
            flops=3 * rows * lanes,
        )
        rows = out_rows - PAD
    readout = call(
        functools.partial(readout_kernel, rows),
        S((owned, width), BF16),
        (keep, got),
        flops=3 * rows * lanes,
    )
    far = far_by(readout)
    near = near_by(readout)
    mid_part = call(
        mid_conv_kernel,
        S((owned, out_width), F32),
        (readout, decode_weight),
        far=(1,),
        scratch=(pltpu.VMEM(half_taps, BF16), dma((1,))),
        flops=conv_flops,
    )
    objects = mask_weight.shape[1]
    logits = call(
        functools.partial(last_kernel, count),
        S((objects, owned), F32),
        (frame_part, mid_part, near, far, end_weight, mask_weight.T),
        flops=2 * conv_flops,
    )
    return logits.T.reshape(query_value.shape[0], query_value.shape[1], objects)


def solution(mesh):
    split = P(("groups", "mem"))
    count = mesh.shape["mem"]

    def step(*args):
        return shards(mesh.shape["groups"], count, *args)

    return jax.shard_map(
        step,
        mesh=mesh,
        in_specs=(split,) * 6 + (P(),) * 3,
        out_specs=split,
        check_vma=False,
    )
```

```python
import functools
import math

import jax
import jax.numpy as jnp
from jax import lax
from jax.experimental import pallas as pl
from jax.experimental.pallas import tpu as pltpu
from jax.sharding import PartitionSpec as P


F32 = jnp.float32
BF16 = jnp.bfloat16
PAD = 16
VM = pl.BlockSpec(memory_space=pltpu.VMEM)
SM = pl.BlockSpec(memory_space=pltpu.SMEM)
HB = pl.BlockSpec(memory_space=pl.ANY)
S = jax.ShapeDtypeStruct
hold = pltpu.with_memory_space_constraint


def call(kernel, out, ins, far=(), scratch=(), flops=0, exps=0):
    size = lambda a: math.prod(a.shape) * jnp.dtype(a.dtype).itemsize
    outs = out if isinstance(out, (tuple, list)) else (out,)
    moved = sum(size(a) for a in ins) + sum(size(a) for a in outs)
    small = lambda a: a.ndim == 1 and a.dtype == jnp.int32
    return pl.pallas_call(
        kernel,
        out_shape=out,
        in_specs=[HB if i in far else SM if small(a) else VM for i, a in enumerate(ins)],
        out_specs=jax.tree.map(lambda _: VM, out),
        scratch_shapes=scratch,
        cost_estimate=pl.CostEstimate(flops=flops, transcendentals=exps, bytes_accessed=moved),
        compiler_params=pltpu.CompilerParams(vmem_limit_bytes=24 << 20),
    )(*[hold(a, pltpu.HBM) if i in far else a for i, a in enumerate(ins)])


def prep_kernel(
    key_hbm, val_hbm, lab_hbm, emb_hbm, q_hbm, count_ref, out_ref, q_ref,
    key_ref, val_ref, lab_ref, emb_ref, sems,
):
    pairs = (
        (val_hbm, val_ref),
        (key_hbm, key_ref),
        (lab_hbm, lab_ref),
        (emb_hbm, emb_ref),
        (q_hbm, q_ref),
    )
    copies = [pltpu.make_async_copy(a, b, sems.at[i]) for i, (a, b) in enumerate(pairs)]
    for copy in copies:
        copy.start()
    pos, width = val_ref.shape
    kwidth = key_ref.shape[1]
    chunk = lab_ref.shape[1]
    objects = emb_ref.shape[0]
    out_ref[...] = jnp.zeros_like(out_ref)
    for copy in copies:
        copy.wait()
    count = count_ref[0]
    live_row = lax.broadcasted_iota(jnp.int32, (pos, kwidth), 0) < count
    keys = key_ref[...].astype(F32)
    keys = jnp.where(live_row, keys, jnp.broadcast_to(keys[0:1], keys.shape))
    out_ref[0:pos, pos : pos + kwidth] = keys.astype(BF16)
    for i in range(pos // chunk):
        ids = jnp.broadcast_to(lab_ref[i : i + 1, :], (objects, chunk))
        onehot = (ids == lax.broadcasted_iota(jnp.int32, (objects, chunk), 0)).astype(F32)
        embedded = lax.dot_general(
            emb_ref[...].astype(F32), onehot, (((0,), (0,)), ((), ())), preferred_element_type=F32
        )
        value = val_ref[i * chunk : (i + 1) * chunk, :].astype(F32).T + embedded
        lane = lax.broadcasted_iota(jnp.int32, (width, chunk), 1) + i * chunk
        value = jnp.where(lane < count, value, 0.0)
        out_ref[0:width, i * chunk : (i + 1) * chunk] = value.astype(BF16)
        tail = lax.broadcasted_iota(jnp.int32, (PAD, chunk), 0)
        lane = lax.broadcasted_iota(jnp.int32, (PAD, chunk), 1) + i * chunk
        out_ref[width : width + PAD, i * chunk : (i + 1) * chunk] = jnp.where(
            (tail == 0) & (lane < count), 1.0, 0.0
        ).astype(BF16)


def pack_tail(peak, mass):
    row = lax.broadcasted_iota(jnp.int32, (PAD, peak.shape[1]), 0)
    high = mass.astype(BF16).astype(F32)
    low = mass - high
    out = jnp.where(row == 0, peak, jnp.where(row == 1, high, jnp.where(row == 2, low, 0.0)))
    return out.astype(BF16)


def keep_tail(peak, mass):
    row = lax.broadcasted_iota(jnp.int32, (PAD, peak.shape[1]), 0)
    return jnp.where(row == 0, peak, jnp.where(row == 1, mass, 0.0))


def attend(blocks, queries, pos, kwidth, width):
    scale = 1.0 / math.sqrt(kwidth)
    parts = []
    for ref in blocks:
        keys = ref[0:pos, pos : pos + kwidth]
        scores = (
            lax.dot_general(keys, queries, (((1,), (1,)), ((), ())), preferred_element_type=F32)
            * scale
        )
        peak = jnp.max(scores, axis=0, keepdims=True)
        weights = jnp.exp(scores - peak).astype(BF16)
        values = jnp.dot(ref[0 : width + PAD, 0:pos], weights, preferred_element_type=F32)
        parts.append((peak, values))
    (peak0, values0), (peak1, values1) = parts
    peak = jnp.maximum(peak0, peak1).astype(BF16).astype(F32)
    values = values0 * jnp.exp(peak0 - peak) + values1 * jnp.exp(peak1 - peak)
    return peak, values


def attend_kernel(pos, kwidth, width, send, mine_ref, other_ref, q_ref, out_ref):
    peak, values = attend((mine_ref, other_ref), q_ref[...], pos, kwidth, width)
    mass = values[width : width + 1]
    out_ref[0:width] = values[0:width].astype(out_ref.dtype)
    out_ref[width : width + PAD] = (pack_tail if send else keep_tail)(peak, mass)


def merged(width, keep_ref, got_ref):
    got_peak = got_ref[width : width + PAD].astype(F32)
    peak, mass = keep_ref[width : width + 1], keep_ref[width + 1 : width + 2]
    got_mass = got_peak[1:2] + got_peak[2:3]
    got_peak = got_peak[0:1]
    top = jnp.maximum(peak, got_peak)
    a, b = jnp.exp(peak - top), jnp.exp(got_peak - top)
    values = keep_ref[0:width] * a + got_ref[0:width].astype(F32) * b
    return values, top, mass * a + got_mass * b


def fold_kernel(width, keep_ref, got_ref, send_out, keep_out):
    values, peak, mass = merged(width, keep_ref, got_ref)
    half = values.shape[1] // 2
    if half % 128 == 0:
        send_out[0:width] = values[:, half:].astype(BF16)
        send_out[width : width + PAD] = pack_tail(peak[:, half:], mass[:, half:])
        keep_out[0:width] = values[:, :half]
        keep_out[width : width + PAD] = keep_tail(peak[:, :half], mass[:, :half])
        return
    rows = width // 2
    low, high = values[0:rows], values[rows:]
    lane = lax.broadcasted_iota(jnp.int32, (1, 2 * half), 1) < half
    swap = lambda x: pltpu.roll(x, half, 1)
    first = lambda x: jnp.where(lane, x, swap(x))
    second = lambda x: jnp.where(lane, swap(x), x)
    peak8, mass8 = (jnp.broadcast_to(x, (8, 2 * half)) for x in (peak, mass))
    send_out[0:rows] = jnp.where(lane, swap(low), high).astype(BF16)
    send_out[rows : rows + PAD] = pack_tail(second(peak8)[0:1], second(mass8)[0:1])
    keep_out[0:rows] = jnp.where(lane, low, swap(high))
    keep_out[rows : rows + PAD] = keep_tail(first(peak8)[0:1], first(mass8)[0:1])


def far_row():
    return 2 - 2 * lax.rem(lax.axis_index("mem"), 2)


def readout_kernel(rows, keep_ref, got_ref, frame_ref, w_ref, out_ref, far_ref):
    values, _, mass = merged(rows, keep_ref, got_ref)
    turned = (values / mass).T
    half = turned.shape[0] // 2
    line = jnp.concatenate([turned[0:half], turned[half:]], axis=1).astype(BF16)
    out_ref[...] = line
    far_ref[...] = frame_ref[...] + taps(line, w_ref)


def rest_kernel(line_ref, frame_ref, w_ref, near_ref, mid_ref):
    line = line_ref[...]
    near_ref[...] = frame_ref[0] + taps(line, w_ref.at[0])
    mid_ref[...] = frame_ref[1] + taps(line, w_ref.at[1])


def join_kernel(a_ref, b_ref, out_ref):
    rows = a_ref.shape[0]
    out_ref[0:rows] = a_ref[...]
    out_ref[rows:] = b_ref[...]


def slide(left, right):
    rows = left.shape[0]
    row = lax.broadcasted_iota(jnp.int32, left.shape, 0)
    left = jnp.where(row == 0, 0.0, pltpu.roll(left, 1, 0))
    right = jnp.where(row == rows - 1, 0.0, pltpu.roll(right, rows - 1, 0))
    return left + right


def taps(line, w_ref):
    left, mid, right = (
        jnp.dot(line, w_ref[col], preferred_element_type=F32) for col in range(3)
    )
    return slide(left, right) + mid


def copy_all(pairs, sems):
    copies = [pltpu.make_async_copy(a, b, sems.at[i]) for i, (a, b) in enumerate(pairs)]
    for copy in copies:
        copy.start()
    return copies


def weight_copies(w_hbm, channels, far_ref, rest_ref):
    far = far_row()
    return [
        (w_hbm.at[far, :, channels], far_ref),
        (w_hbm.at[2 - far, :, channels], rest_ref.at[0]),
        (w_hbm.at[1, :, channels], rest_ref.at[1]),
    ]


def frame_kernel(frame_hbm, w_hbm, far_ref, rest_ref, frame_ref, wfar_ref, wrest_ref, sems):
    width = frame_ref.shape[1]
    pairs = weight_copies(w_hbm, pl.ds(width, width), wfar_ref, wrest_ref)
    copies = copy_all([(frame_hbm, frame_ref)] + pairs, sems)
    copies[0].wait()
    copies[1].wait()
    line = frame_ref[...]
    far_ref[...] = taps(line, wfar_ref)
    for i in range(2):
        copies[2 + i].wait()
        rest_ref[i] = taps(line, wrest_ref.at[i])


def stage_kernel(w_hbm, far_ref, rest_ref, sems):
    low = pl.ds(0, far_ref.shape[1])
    for copy in copy_all(weight_copies(w_hbm, low, far_ref, rest_ref), sems):
        copy.wait()


def last_kernel(count, mid_ref, near_ref, far_ref, mask_ref, out_ref):
    place = lax.axis_index("mem")
    far = far_ref[...]
    far = jnp.where((place == 0) | (place == count - 1), jnp.zeros_like(far), far)
    hidden = jnp.maximum(mid_ref[...] + near_ref[...] + far, 0.0).astype(BF16)
    out_ref[...] = lax.dot_general(
        mask_ref[...], hidden, (((1,), (1,)), ((), ())), preferred_element_type=F32
    )


def shards(
    groups,
    count,
    mem_key,
    value_base,
    memory_labels,
    valid_counts,
    query_key,
    query_value,
    object_embed,
    decode_weight,
    mask_weight,
):
    kwidth, width = mem_key.shape[2], value_base.shape[2]
    pos = mem_key.shape[0] * mem_key.shape[1]
    tall = max(pos, width) + PAD
    owned = query_value.shape[0] * query_value.shape[1]
    out_width = decode_weight.shape[3]

    steps = count.bit_length() - 2
    order = [1 << i for i in range(1, steps + 1)]
    order[0:2] = order[1::-1]

    def swap(x, step):
        return lax.ppermute(x, "mem", [(i, i ^ order[step]) for i in range(count)])

    def near_by(x):
        return lax.ppermute(x, "mem", [(i, i ^ 1) for i in range(count)])

    def far_by(x):
        links = []
        for group in range(groups):
            base = group * count
            links += [(base + i, base + i + 1) for i in range(1, count - 1, 2)]
            if groups % 2 == 0 and group % 2 == 0:
                links += [(base + i, base + count + i) for i in (0, count - 1)]
        links += [(b, a) for a, b in links]
        return lax.ppermute(x, ("groups", "mem"), links)

    queries = query_key.reshape(owned, kwidth)
    frame = query_value.reshape(owned, width)
    dma = pltpu.SemaphoreType.DMA
    got = swap(queries, steps - 1)
    mine, queries = call(
        prep_kernel,
        (S((tall, pos + kwidth), BF16), S(queries.shape, BF16)),
        (
            mem_key.reshape(pos, kwidth),
            value_base.reshape(pos, width),
            memory_labels,
            object_embed,
            queries,
            valid_counts,
        ),
        far=range(5),
        scratch=(
            pltpu.VMEM((pos, kwidth), BF16),
            pltpu.VMEM((pos, width), BF16),
            pltpu.VMEM(memory_labels.shape, jnp.int32),
            pltpu.VMEM(object_embed.shape, BF16),
            dma((5,)),
        ),
        flops=2 * pos * width * 8,
    )
    other = near_by(mine)

    for i in range(steps - 1):
        queries = call(
            join_kernel, S((2 * queries.shape[0], kwidth), BF16), (queries, got)
        )
        got = swap(queries, steps - 2 - i)
    theirs = got

    lanes = queries.shape[0]
    work = dict(flops=4 * lanes * pos * (kwidth + width), exps=2 * lanes * pos)
    attend_call = lambda q, send, dtype: call(
        functools.partial(attend_kernel, pos, kwidth, width, send),
        S((width + PAD, lanes), dtype),
        (mine, other, q),
        **work,
    )
    keep = attend_call(queries, False, F32)
    send = attend_call(theirs, True, BF16)
    conv_flops = 2 * owned * width * out_width * 3
    half_taps = (decode_weight.shape[1], width, out_width)
    plane = (owned, out_width)
    frame_far, frame_rest = call(
        frame_kernel,
        (S(plane, F32), S((2, *plane), F32)),
        (frame, decode_weight),
        far=(0, 1),
        scratch=(
            pltpu.VMEM(frame.shape, BF16),
            pltpu.VMEM(half_taps, BF16),
            pltpu.VMEM((2, *half_taps), BF16),
            dma((4,)),
        ),
        flops=3 * conv_flops,
    )
    far_weight, rest_weight = call(
        stage_kernel,
        (S(half_taps, BF16), S((2, *half_taps), BF16)),
        (decode_weight,),
        far=(0,),
        scratch=(dma((3,)),),
    )
    rows = width
    for i in range(steps):
        got = swap(send, i)
        if i + 1 == steps:
            break
        lanes = lanes // 2
        if lanes % 128:
            out_rows, out_lanes = rows // 2 + PAD, 2 * lanes
        else:
            out_rows, out_lanes = rows + PAD, lanes
        send, keep = call(
            functools.partial(fold_kernel, rows),
            (S((out_rows, out_lanes), BF16), S((out_rows, out_lanes), F32)),
            (keep, got),
            flops=3 * rows * lanes,
        )
        rows = out_rows - PAD
    readout, far = call(
        functools.partial(readout_kernel, rows),
        (S((owned, width), BF16), S(plane, F32)),
        (keep, got, frame_far, far_weight),
        flops=conv_flops,
    )
    far = far_by(far)
    near, middle = call(
        rest_kernel,
        (S(plane, F32), S(plane, F32)),
        (readout, frame_rest, rest_weight),
        flops=2 * conv_flops,
    )
    near = near_by(near)
    objects = mask_weight.shape[1]
    logits = call(
        functools.partial(last_kernel, count),
        S((objects, owned), F32),
        (middle, near, far, mask_weight.T),
        flops=2 * owned * out_width * objects,
    )
    return logits.T.reshape(query_value.shape[0], query_value.shape[1], objects)


def solution(mesh):
    split = P(("groups", "mem"))
    count = mesh.shape["mem"]

    def step(*args):
        return shards(mesh.shape["groups"], count, *args)

    return jax.shard_map(
        step,
        mesh=mesh,
        in_specs=(split,) * 6 + (P(),) * 3,
        out_specs=split,
        check_vma=False,
    )
```

```python
import functools
import math

import jax
import jax.numpy as jnp
from jax import lax
from jax.experimental import pallas as pl
from jax.experimental.pallas import tpu as pltpu
from jax.sharding import PartitionSpec as P


F32 = jnp.float32
BF16 = jnp.bfloat16
PAD = 16
BLOCK = 128
VM = pl.BlockSpec(memory_space=pltpu.VMEM)
SM = pl.BlockSpec(memory_space=pltpu.SMEM)
HB = pl.BlockSpec(memory_space=pl.ANY)
S = jax.ShapeDtypeStruct
hold = pltpu.with_memory_space_constraint


def call(kernel, out, ins, far=(), scratch=(), flops=0, exps=0):
    size = lambda a: math.prod(a.shape) * jnp.dtype(a.dtype).itemsize
    outs = out if isinstance(out, (tuple, list)) else (out,)
    moved = sum(size(a) for a in ins) + sum(size(a) for a in outs)
    small = lambda a: a.ndim == 1 and a.dtype == jnp.int32
    return pl.pallas_call(
        kernel,
        out_shape=out,
        in_specs=[HB if i in far else SM if small(a) else VM for i, a in enumerate(ins)],
        out_specs=jax.tree.map(lambda _: VM, out),
        scratch_shapes=scratch,
        cost_estimate=pl.CostEstimate(flops=flops, transcendentals=exps, bytes_accessed=moved),
        compiler_params=pltpu.CompilerParams(vmem_limit_bytes=24 << 20),
    )(*[hold(a, pltpu.HBM) if i in far else a for i, a in enumerate(ins)])


def prep_kernel(
    key_hbm, val_hbm, lab_hbm, emb_hbm, q_hbm, count_ref, out_ref, q_ref,
    key_ref, val_ref, lab_ref, emb_ref, sems,
):
    pairs = (
        (val_hbm, val_ref),
        (key_hbm, key_ref),
        (lab_hbm, lab_ref),
        (emb_hbm, emb_ref),
        (q_hbm, q_ref),
    )
    copies = [pltpu.make_async_copy(a, b, sems.at[i]) for i, (a, b) in enumerate(pairs)]
    for copy in copies:
        copy.start()
    pos, width = val_ref.shape
    kwidth = key_ref.shape[1]
    chunk = lab_ref.shape[1]
    objects = emb_ref.shape[0]
    out_ref[...] = jnp.zeros_like(out_ref)
    for copy in copies:
        copy.wait()
    count = count_ref[0]
    live_row = lax.broadcasted_iota(jnp.int32, (pos, kwidth), 0) < count
    keys = key_ref[...].astype(F32)
    keys = jnp.where(live_row, keys, jnp.broadcast_to(keys[0:1], keys.shape))
    out_ref[0:pos, pos : pos + kwidth] = keys.astype(BF16)
    for i in range(pos // chunk):
        ids = jnp.broadcast_to(lab_ref[i : i + 1, :], (objects, chunk))
        onehot = (ids == lax.broadcasted_iota(jnp.int32, (objects, chunk), 0)).astype(F32)
        embedded = lax.dot_general(
            emb_ref[...].astype(F32), onehot, (((0,), (0,)), ((), ())), preferred_element_type=F32
        )
        value = val_ref[i * chunk : (i + 1) * chunk, :].astype(F32).T + embedded
        lane = lax.broadcasted_iota(jnp.int32, (width, chunk), 1) + i * chunk
        value = jnp.where(lane < count, value, 0.0)
        out_ref[0:width, i * chunk : (i + 1) * chunk] = value.astype(BF16)
        tail = lax.broadcasted_iota(jnp.int32, (PAD, chunk), 0)
        lane = lax.broadcasted_iota(jnp.int32, (PAD, chunk), 1) + i * chunk
        out_ref[width : width + PAD, i * chunk : (i + 1) * chunk] = jnp.where(
            (tail == 0) & (lane < count), 1.0, 0.0
        ).astype(BF16)


def pack_tail(peak, mass):
    row = lax.broadcasted_iota(jnp.int32, (PAD, peak.shape[1]), 0)
    high = mass.astype(BF16).astype(F32)
    low = mass - high
    out = jnp.where(row == 0, peak, jnp.where(row == 1, high, jnp.where(row == 2, low, 0.0)))
    return out.astype(BF16)


def keep_tail(peak, mass):
    row = lax.broadcasted_iota(jnp.int32, (PAD, peak.shape[1]), 0)
    return jnp.where(row == 0, peak, jnp.where(row == 1, mass, 0.0))


def attend(blocks, queries, pos, kwidth, width):
    scale = 1.0 / math.sqrt(kwidth)
    parts = []
    for ref in blocks:
        keys = ref[0:pos, pos : pos + kwidth]
        scores = (
            lax.dot_general(keys, queries, (((1,), (1,)), ((), ())), preferred_element_type=F32)
            * scale
        )
        peak = jnp.max(scores, axis=0, keepdims=True)
        weights = jnp.exp(scores - peak).astype(BF16)
        values = jnp.dot(ref[0 : width + PAD, 0:pos], weights, preferred_element_type=F32)
        parts.append((peak, values))
    (peak0, values0), (peak1, values1) = parts
    peak = jnp.maximum(peak0, peak1).astype(BF16).astype(F32)
    values = values0 * jnp.exp(peak0 - peak) + values1 * jnp.exp(peak1 - peak)
    return peak, values


def attend_kernel(pos, kwidth, width, send, mine_ref, other_ref, q_ref, out_ref):
    starts = range(BLOCK * send, q_ref.shape[0], 2 * BLOCK)
    queries = [q_ref[i : i + BLOCK] for i in starts]
    queries = queries[0] if len(queries) == 1 else jnp.concatenate(queries, axis=0)
    peak, values = attend((mine_ref, other_ref), queries, pos, kwidth, width)
    mass = values[width : width + 1]
    out_ref[0:width] = values[0:width].astype(out_ref.dtype)
    out_ref[width : width + PAD] = (pack_tail if send else keep_tail)(peak, mass)


def merged(width, keep_ref, got_ref):
    got_peak = got_ref[width : width + PAD].astype(F32)
    peak, mass = keep_ref[width : width + 1], keep_ref[width + 1 : width + 2]
    got_mass = got_peak[1:2] + got_peak[2:3]
    got_peak = got_peak[0:1]
    top = jnp.maximum(peak, got_peak)
    a, b = jnp.exp(peak - top), jnp.exp(got_peak - top)
    values = keep_ref[0:width] * a + got_ref[0:width].astype(F32) * b
    return values, top, mass * a + got_mass * b


def put(width, send_out, keep_out, sent, kept):
    send_out[0:width] = sent[0].astype(BF16)
    send_out[width : width + PAD] = pack_tail(*sent[1:])
    keep_out[0:width] = kept[0]
    keep_out[width : width + PAD] = keep_tail(*kept[1:])


def first_fold_kernel(width, keep0_ref, got0_ref, keep1_ref, got1_ref, send_out, keep_out):
    early = merged(width, keep0_ref, got0_ref)
    late = merged(width, keep1_ref, got1_ref)
    half = BLOCK // 2
    lane = lax.broadcasted_iota(jnp.int32, (1, BLOCK), 1) < half
    kept, sent = [], []
    for a, b in zip(early, late, strict=True):
        rows = a.shape[0]
        wide = max(rows, 8)
        a, b = (jnp.broadcast_to(x, (wide, x.shape[1])) for x in (a, b))
        low, high = [], []
        for i in range(0, a.shape[1], BLOCK):
            left, right = a[:, i : i + BLOCK], b[:, i : i + BLOCK]
            low.append(jnp.where(lane, left, pltpu.roll(right, half, 1)))
            high.append(jnp.where(lane, pltpu.roll(left, half, 1), right))
        join = lambda xs: (xs[0] if len(xs) == 1 else jnp.concatenate(xs, axis=1))[0:rows]
        kept.append(join(low))
        sent.append(join(high))
    put(width, send_out, keep_out, sent, kept)


def fold_kernel(width, keep_ref, got_ref, send_out, keep_out):
    values, peak, mass = merged(width, keep_ref, got_ref)
    half = values.shape[1] // 2
    if half % BLOCK == 0:
        sent, kept = (tuple(x[:, i : i + half] for x in (values, peak, mass)) for i in (half, 0))
        put(width, send_out, keep_out, sent, kept)
        return
    rows = width // 2
    low, high = values[0:rows], values[rows:]
    lane = lax.broadcasted_iota(jnp.int32, (1, 2 * half), 1) < half
    swap = lambda x: pltpu.roll(x, half, 1)
    peak8, mass8 = (jnp.broadcast_to(x, (8, 2 * half)) for x in (peak, mass))
    second = lambda x: jnp.where(lane, swap(x), x)[0:1]
    first = lambda x: jnp.where(lane, x, swap(x))[0:1]
    sent = (jnp.where(lane, swap(low), high), second(peak8), second(mass8))
    kept = (jnp.where(lane, low, swap(high)), first(peak8), first(mass8))
    put(rows, send_out, keep_out, sent, kept)


def far_row():
    return 2 - 2 * lax.rem(lax.axis_index("mem"), 2)


def readout_kernel(rows, keep_ref, got_ref, frame_ref, w_ref, out_ref, far_ref):
    values, _, mass = merged(rows, keep_ref, got_ref)
    turned = (values / mass).T
    half = turned.shape[0] // 2
    line = jnp.concatenate([turned[0:half], turned[half:]], axis=1).astype(BF16)
    out_ref[...] = line
    far_ref[...] = frame_ref[...] + taps(line, w_ref)


def rest_kernel(line_ref, frame_ref, w_ref, near_ref, mid_ref):
    line = line_ref[...]
    near_ref[...] = frame_ref[0] + taps(line, w_ref.at[0])
    mid_ref[...] = frame_ref[1] + taps(line, w_ref.at[1])


def join_kernel(a_ref, b_ref, out_ref):
    rows = a_ref.shape[0]
    out_ref[0:rows] = a_ref[...]
    out_ref[rows:] = b_ref[...]


def slide(left, right):
    rows = left.shape[0]
    row = lax.broadcasted_iota(jnp.int32, left.shape, 0)
    left = jnp.where(row == 0, 0.0, pltpu.roll(left, 1, 0))
    right = jnp.where(row == rows - 1, 0.0, pltpu.roll(right, rows - 1, 0))
    return left + right


def taps(line, w_ref):
    left, mid, right = (
        jnp.dot(line, w_ref[col], preferred_element_type=F32) for col in range(3)
    )
    return slide(left, right) + mid


def copy_all(pairs, sems):
    copies = [pltpu.make_async_copy(a, b, sems.at[i]) for i, (a, b) in enumerate(pairs)]
    for copy in copies:
        copy.start()
    return copies


def weight_copies(w_hbm, channels, far_ref, rest_ref):
    far = far_row()
    return [
        (w_hbm.at[far, :, channels], far_ref),
        (w_hbm.at[2 - far, :, channels], rest_ref.at[0]),
        (w_hbm.at[1, :, channels], rest_ref.at[1]),
    ]


def frame_kernel(frame_hbm, w_hbm, far_ref, rest_ref, frame_ref, wfar_ref, wrest_ref, sems):
    width = frame_ref.shape[1]
    pairs = weight_copies(w_hbm, pl.ds(width, width), wfar_ref, wrest_ref)
    copies = copy_all([(frame_hbm, frame_ref)] + pairs, sems)
    copies[0].wait()
    copies[1].wait()
    line = frame_ref[...]
    far_ref[...] = taps(line, wfar_ref)
    for i in range(2):
        copies[2 + i].wait()
        rest_ref[i] = taps(line, wrest_ref.at[i])


def stage_kernel(w_hbm, far_ref, rest_ref, sems):
    low = pl.ds(0, far_ref.shape[1])
    for copy in copy_all(weight_copies(w_hbm, low, far_ref, rest_ref), sems):
        copy.wait()


def last_kernel(count, mid_ref, near_ref, far_ref, mask_ref, out_ref):
    place = lax.axis_index("mem")
    far = far_ref[...]
    far = jnp.where((place == 0) | (place == count - 1), jnp.zeros_like(far), far)
    hidden = jnp.maximum(mid_ref[...] + near_ref[...] + far, 0.0).astype(BF16)
    out_ref[...] = lax.dot_general(
        mask_ref[...], hidden, (((1,), (1,)), ((), ())), preferred_element_type=F32
    )


def shards(
    groups,
    count,
    mem_key,
    value_base,
    memory_labels,
    valid_counts,
    query_key,
    query_value,
    object_embed,
    decode_weight,
    mask_weight,
):
    kwidth, width = mem_key.shape[2], value_base.shape[2]
    pos = mem_key.shape[0] * mem_key.shape[1]
    tall = max(pos, width) + PAD
    owned = query_value.shape[0] * query_value.shape[1]
    out_width = decode_weight.shape[3]

    gathers = [1 << i for i in range(1, count.bit_length() - 1)]
    reduces = [gathers[1], gathers[0], *gathers[2:]]

    def swap(x, mask):
        return lax.ppermute(x, "mem", [(i, i ^ mask) for i in range(count)])

    def near_by(x):
        return lax.ppermute(x, "mem", [(i, i ^ 1) for i in range(count)])

    def far_by(x):
        links = []
        for group in range(groups):
            base = group * count
            links += [(base + i, base + i + 1) for i in range(1, count - 1, 2)]
            if groups % 2 == 0 and group % 2 == 0:
                links += [(base + i, base + count + i) for i in (0, count - 1)]
        links += [(b, a) for a, b in links]
        return lax.ppermute(x, ("groups", "mem"), links)

    queries = query_key.reshape(owned, kwidth)
    frame = query_value.reshape(owned, width)
    dma = pltpu.SemaphoreType.DMA
    got = swap(queries, gathers[0])
    mine, queries = call(
        prep_kernel,
        (S((tall, pos + kwidth), BF16), S(queries.shape, BF16)),
        (
            mem_key.reshape(pos, kwidth),
            value_base.reshape(pos, width),
            memory_labels,
            object_embed,
            queries,
            valid_counts,
        ),
        far=range(5),
        scratch=(
            pltpu.VMEM((pos, kwidth), BF16),
            pltpu.VMEM((pos, width), BF16),
            pltpu.VMEM(memory_labels.shape, jnp.int32),
            pltpu.VMEM(object_embed.shape, BF16),
            dma((5,)),
        ),
        flops=2 * pos * width * 8,
    )
    other = near_by(mine)

    for mask in gathers[1:]:
        queries = call(
            join_kernel, S((2 * queries.shape[0], kwidth), BF16), (queries, got)
        )
        got = swap(queries, mask)

    lanes = queries.shape[0] // 2
    keeps, gots = [], []
    for block in (queries, got):
        sides = []
        for send, dtype in ((1, BF16), (0, F32)):
            sides.append(
                call(
                    functools.partial(attend_kernel, pos, kwidth, width, send),
                    S((width + PAD, lanes), dtype),
                    (mine, other, block),
                    flops=4 * lanes * pos * (kwidth + width),
                    exps=2 * lanes * pos,
                )
            )
        gots.append(swap(sides[0], reduces[0]))
        keeps.append(sides[1])
    conv_flops = 2 * owned * width * out_width * 3
    half_taps = (decode_weight.shape[1], width, out_width)
    plane = (owned, out_width)
    frame_far, frame_rest = call(
        frame_kernel,
        (S(plane, F32), S((2, *plane), F32)),
        (frame, decode_weight),
        far=(0, 1),
        scratch=(
            pltpu.VMEM(frame.shape, BF16),
            pltpu.VMEM(half_taps, BF16),
            pltpu.VMEM((2, *half_taps), BF16),
            dma((4,)),
        ),
        flops=3 * conv_flops,
    )
    far_weight, rest_weight = call(
        stage_kernel,
        (S(half_taps, BF16), S((2, *half_taps), BF16)),
        (decode_weight,),
        far=(0,),
        scratch=(dma((3,)),),
    )
    send, keep = call(
        functools.partial(first_fold_kernel, width),
        (S((width + PAD, lanes), BF16), S((width + PAD, lanes), F32)),
        (keeps[0], gots[0], keeps[1], gots[1]),
        flops=6 * width * lanes,
    )
    rows = width
    for mask in reduces[1:]:
        got = swap(send, mask)
        if mask == reduces[-1]:
            break
        lanes = lanes // 2
        if lanes % BLOCK:
            out_rows, out_lanes = rows // 2 + PAD, 2 * lanes
        else:
            out_rows, out_lanes = rows + PAD, lanes
        send, keep = call(
            functools.partial(fold_kernel, rows),
            (S((out_rows, out_lanes), BF16), S((out_rows, out_lanes), F32)),
            (keep, got),
            flops=3 * rows * lanes,
        )
        rows = out_rows - PAD
    readout, far = call(
        functools.partial(readout_kernel, rows),
        (S((owned, width), BF16), S(plane, F32)),
        (keep, got, frame_far, far_weight),
        flops=conv_flops,
    )
    far = far_by(far)
    near, middle = call(
        rest_kernel,
        (S(plane, F32), S(plane, F32)),
        (readout, frame_rest, rest_weight),
        flops=2 * conv_flops,
    )
    near = near_by(near)
    objects = mask_weight.shape[1]
    logits = call(
        functools.partial(last_kernel, count),
        S((objects, owned), F32),
        (middle, near, far, mask_weight.T),
        flops=2 * owned * out_width * objects,
    )
    return logits.T.reshape(query_value.shape[0], query_value.shape[1], objects)


def solution(mesh):
    split = P(("groups", "mem"))
    count = mesh.shape["mem"]

    def step(*args):
        return shards(mesh.shape["groups"], count, *args)

    return jax.shard_map(
        step,
        mesh=mesh,
        in_specs=(split,) * 6 + (P(),) * 3,
        out_specs=split,
        check_vma=False,
    )
```
